256 devices in a mesh: row: 8 (over x, core), col: 32 (over y, z).
Axes of the slice: x: 4, y: 4, z: 8, core: 2. Of those that a mesh axis runs over, the one named last changes fastest.
Arguments:
- response: float32 [18432, 18432], P('row', 'col'), may hold values from 0.002 to 0.02
- tile_map: int32 [288, 288], P('row', 'col'), may hold values 0 or 1
- band_offsets: int32 [288, 2], P('row'), may hold values from -48 to 48, as said below
- prior_spectra: float32 [512, 18432], P(None, 'col'), may hold values from 0.5 to 2
- boot_counts: int32 [512, 18432], P('col', 'row'), may hold values from 0 to 3
- spectrum: float32 [18432], P('row'), may hold values from 5 to 50
Outputs:
- covariance: float32 [18432, 18432], P('row', 'col')
- unfolded: float32 [512, 18432], P(None, 'col')
The draws below stay inside these ranges and needn't reach their ends.
Inputs may be any that keep to these rules, and one draw needn't show every extreme that they name: `band_offsets`: column 0 is at most 0 and column 1 at least 0; some tile row reaches -48 and some reaches 48.
All inputs are finite; a program needn't handle non-finite values. No bound on the sum of `tile_map` on one device may be relied on, other than what follows from the above.
Results may differ from the reference program's by a relative error of at most 0.0003.
Values sent between devices are 32-bit elements; how exact they have to be, the bound alone decides.
A program may use at most 64 MiB of HBM per device.

```python
import math
import jax
import jax.numpy as jnp
from jax import lax

NB = 18432
TILE = 64
REACH = 48
NR = 512
NT = 288
N_ROW = 8


def draw_band_offsets(key, part):
    lower_key, upper_key = jax.random.split(jax.random.fold_in(key, 17))
    lower_reach = -jax.random.randint(lower_key, (NT,), 0, REACH + 1)
    upper_reach = jax.random.randint(upper_key, (NT,), 0, REACH + 1)
    lower_reach = lower_reach.at[1].set(-REACH)
    upper_reach = upper_reach.at[0].set(REACH)
    return jnp.stack([lower_reach, upper_reach], axis=1).astype(jnp.int32)


def set_ends(array, key, low, high):
    index_at = [jax.random.randint(jax.random.fold_in(key, axis), (), 0, length) for axis, length in enumerate(array.shape)]
    longest = array.shape.index(max(array.shape))
    next_to = index_at[:longest] + [(index_at[longest] + 1) % array.shape[longest]] + index_at[longest + 1:]
    return array.at[tuple(index_at)].set(low).at[tuple(next_to)].set(high)


def block_scale(rng, shape, cuts, low, top_value):
    factor_of, own = 1.0, jax.random.fold_in(rng, 6)
    for dim, parts in cuts:
        draws = jnp.exp(jax.random.uniform(jax.random.fold_in(own, dim), (parts,), jnp.float32, low / len(cuts), top_value / len(cuts)))
        factor_of = factor_of * jnp.repeat(draws, shape[dim] // parts).reshape([-1 if axis == dim else 1 for axis in range(len(shape))])
    return factor_of


def setup_inputs(seed: int = 0) -> dict:
    splits = jax.random.split(jax.random.key(seed), 7)
    response = jnp.clip(jnp.exp(math.log(0.02) - 2.30258502 * jax.random.uniform(splits[0], (NB, NB), jnp.float32) ** block_scale(splits[0], (NB, NB), ((0, 8), (1, 32)), -0.2, 0.2)), 0.002, 0.02)
    tile_map = set_ends((jax.random.randint(splits[1], (NT, NT), 0, 4) < 3).astype(jnp.int32), jax.random.fold_in(splits[1], 1), 0, 1)
    band_offsets = draw_band_offsets(jax.random.fold_in(splits[6], 71), 0)
    prior_spectra = jnp.clip(jnp.exp(math.log(2.0) - 1.3862944 * jax.random.uniform(splits[3], (NR, NB), jnp.float32) ** block_scale(splits[3], (NR, NB), ((1, 32),), -0.2, 0.2)), 0.5, 2.0)
    boot_counts = set_ends(jax.random.randint(splits[4], (NR, NB), 0, 4), jax.random.fold_in(splits[4], 1), 0, 3).astype(jnp.int32)
    spectrum = jnp.clip(jnp.exp(math.log(50.0) - 2.3025851 * jax.random.uniform(splits[5], (NB,), jnp.float32) ** block_scale(splits[5], (NB,), ((0, 8),), -0.2, 0.2)), 5.0, 50.0)
    return {"response": response, "tile_map": tile_map, "band_offsets": band_offsets, "prior_spectra": prior_spectra, "boot_counts": boot_counts, "spectrum": spectrum}


def kept_tiles(tile_rows, offset_rows, first_tile, tile_count):
    measured = first_tile + jnp.arange(tile_count, dtype=jnp.int32)[:, None]
    truth = jnp.arange(tile_rows.shape[1], dtype=jnp.int32)[None, :]
    inside = (truth >= measured + offset_rows[:, 0:1]) & (truth <= measured + offset_rows[:, 1:2])
    return (truth == measured) | (inside & (tile_rows == 1))


def reference(response, tile_map, band_offsets, prior_spectra, boot_counts, spectrum):
    block_bins = NB // N_ROW
    block_tiles = block_bins // TILE

    def fold_block(state_pair, block_index):
        back_sum, column_sums = state_pair
        first_bin = (block_index * block_bins).astype(jnp.int32)
        first_tile = (block_index * block_tiles).astype(jnp.int32)
        response_rows = lax.dynamic_slice_in_dim(response, first_bin, block_bins, 0)
        tile_rows = lax.dynamic_slice_in_dim(tile_map, first_tile, block_tiles, 0)
        offset_rows = lax.dynamic_slice_in_dim(band_offsets, first_tile, block_tiles, 0)
        kept = kept_tiles(tile_rows, offset_rows, first_tile, block_tiles)
        expanded = jnp.repeat(jnp.repeat(kept, TILE, 0), TILE, 1)
        masked = jnp.where(expanded, response_rows, jnp.zeros_like(response_rows))
        folded = jnp.dot(prior_spectra, masked.T, precision=lax.Precision.HIGHEST, preferred_element_type=jnp.float32)
        weights = lax.dynamic_slice_in_dim(boot_counts, first_bin, block_bins, 1).astype(jnp.float32)
        measured = lax.dynamic_slice_in_dim(spectrum, first_bin, block_bins, 0)
        ratios = weights * measured[None, :] / folded
        back_sum = back_sum + jnp.dot(ratios, masked, precision=lax.Precision.HIGHEST, preferred_element_type=jnp.float32)
        column_sums = column_sums + jnp.sum(masked, axis=0)
        return (back_sum, column_sums), None

    start_state = (jnp.zeros((NR, NB), jnp.float32), jnp.zeros((NB,), jnp.float32))
    (back_sum, efficiency), _ = lax.scan(fold_block, start_state, jnp.arange(N_ROW, dtype=jnp.int32))
    unfolded = prior_spectra * back_sum / efficiency[None, :]
    centred = unfolded - jnp.mean(unfolded, axis=0)[None, :]
    covariance = jnp.dot(centred.T, centred, precision=lax.Precision.HIGHEST, preferred_element_type=jnp.float32) / (NR - 1)
    return covariance, unfolded
```

```python
import functools

import jax
import jax.numpy as jnp
from jax import lax
from jax.experimental import pallas as pl
from jax.experimental.pallas import tpu as pltpu
from jax.sharding import Mesh
from jax.sharding import PartitionSpec as P

COL = ("col_0", "col_1")
NY, NZ = 4, 8
AXES = {"col_0": NY, "col_1": NZ}
BY_MESH = pl.DeviceIdType.MESH
DIRS = (1, -1)


def wrap(v, n):
    return lax.rem(v + 2 * n, n)


def part_of(direction):
    return 0 if direction == 1 else 1


def greet(devices):
    barrier = pltpu.get_barrier_semaphore()
    for device in devices:
        pl.semaphore_signal(barrier, inc=1, device_id=device, device_id_type=BY_MESH)
    pl.semaphore_wait(barrier, len(devices))


def offset(axis, v):
    return (v, 0) if axis == "col_0" else (0, v)


def plus(a, b):
    return (a[0] + b[0], a[1] + b[1])


def tree():
    stages = []
    for half, (a, b) in enumerate((("col_1", "col_0"), ("col_0", "col_1"))):
        na, nb = AXES[a], AXES[b]

        def onward(axis, direction, shard, step, half=half):
            last = AXES[axis] // 2
            if step >= last:
                return []
            there = plus(shard, offset(axis, -direction))
            return [(half, axis, direction, there, part_of(direction) if step + 1 == last else 2)]

        def branch(shard, half=half, b=b):
            return [(half, b, d, plus(shard, offset(b, -d)), 2) for d in DIRS]

        own = (0, 0)
        stages.append((0, 0, [], [(half, a, d, offset(a, -d), 2) for d in DIRS] + branch(own)))
        for t in range(1, na // 2 + 1):
            if t < na // 2:
                for d in DIRS:
                    key = (half, a, d, offset(a, -d * t), 2)
                    stages.append((t, 1, [key], onward(a, d, key[3], t) + branch(key[3])))
            else:
                keys = [(half, a, d, offset(a, -d * t), part_of(d)) for d in DIRS]
                stages.append((t, 1, keys, branch(offset(a, t))))
        for e in range(-(na // 2) + 1, na // 2 + 1):
            for t in range(1, nb // 2 + 1):
                for d in DIRS:
                    shard = plus(offset(a, e), offset(b, -d * t))
                    key = (half, b, d, shard, 2 if t < nb // 2 else part_of(d))
                    stages.append((abs(e) + t, 2, [key], onward(b, d, shard, t)))
    return stages


def canonical(key):
    half, axis, d, (dy, dz), part = key
    return (half, axis, d, (dy % NY, dz % NZ), part)


STAGES = [
    (r, s, [canonical(k) for k in waits], [canonical(k) for k in starts])
    for r, s, waits, starts in tree()
]
KEYS = sorted({k for _, _, waits, _ in STAGES for k in waits})
INDEX = {k: i for i, k in enumerate(KEYS)}


def columns(part, width):
    return {0: pl.ds(0, width // 2), 1: pl.ds(width // 2, width // 2), 2: pl.ds(0, width)}[part]


class Plane:
    def __init__(self):
        self.y, self.z = lax.axis_index("col_0"), lax.axis_index("col_1")

    def slot(self, shard):
        return wrap(self.y + shard[0], NY) * NZ + wrap(self.z + shard[1], NZ)

    def neighbour(self, axis, d):
        me = self.y if axis == "col_0" else self.z
        return {axis: wrap(me + d, AXES[axis])}

    def greet(self):
        greet([self.neighbour(axis, d) for axis in AXES for d in DIRS])


def gather_kernel(x, out, send, recv):
    plane = Plane()
    width = x.shape[-1]
    plane.greet()

    def copy_in(key):
        half, axis, d, shard, part = key
        here = out.at[plane.slot(shard), half, :, columns(part, width)]
        i = INDEX[key]
        return pltpu.make_async_remote_copy(
            src_ref=here, dst_ref=here, send_sem=send.at[i], recv_sem=recv.at[i],
            device_id=plane.neighbour(axis, -d), device_id_type=BY_MESH,
        )

    def copy_out(key):
        half, axis, d, shard, part = key
        shard = plus(shard, offset(axis, d))
        shard = (shard[0] % NY, shard[1] % NZ)
        cols = columns(part, width)
        there = out.at[plane.slot(shard), half, :, cols]
        src = x.at[half, :, cols] if shard == (0, 0) else there
        i = INDEX[key]
        return pltpu.make_async_remote_copy(
            src_ref=src, dst_ref=there, send_sem=send.at[i], recv_sem=recv.at[i],
            device_id=plane.neighbour(axis, d), device_id_type=BY_MESH,
        )

    started = []
    last = []
    order = sorted(STAGES, key=lambda s: (s[0], s[1]))
    for _, _, waits, starts in order:
        if waits and not starts:
            last.append(waits)
            continue
        for key in waits:
            copy_in(key).wait_recv()
        for key in starts:
            copy = copy_out(key)
            copy.start()
            started.append(copy)
    for half in range(2):
        out[plane.slot((0, 0)), half] = x[half]
    for waits in last:
        for key in waits:
            copy_in(key).wait_recv()
    for copy in started:
        copy.wait_send()


def plane_gather(x, collective_id):
    rows, width = x.shape
    n = len(KEYS)
    out = pl.pallas_call(
        gather_kernel,
        out_shape=jax.ShapeDtypeStruct((NY * NZ, 2, rows // 2, width), x.dtype),
        in_specs=[pl.BlockSpec(memory_space=pltpu.VMEM)],
        out_specs=pl.BlockSpec(memory_space=pltpu.VMEM),
        scratch_shapes=[pltpu.SemaphoreType.DMA((n,)), pltpu.SemaphoreType.DMA((n,))],
        compiler_params=pltpu.CompilerParams(
            collective_id=collective_id, has_side_effects=True, vmem_limit_bytes=48 << 20
        ),
        name="plane_gather",
    )(x.reshape(2, rows // 2, width))
    return out.reshape(NY * NZ * rows, width)


def scatter_kernel(x, out, got, work, send, recv):
    plane = Plane()
    width = x.shape[-1]
    plane.greet()

    def send_of(key, src):
        half, axis, d, shard, part = key
        i = INDEX[key]
        there = got.at[i, :, columns(part, width)]
        return pltpu.make_async_remote_copy(
            src_ref=src, dst_ref=there, send_sem=send.at[i], recv_sem=recv.at[i],
            device_id=plane.neighbour(axis, -d), device_id_type=BY_MESH,
        )

    def recv_of(key):
        half, axis, d, shard, part = key
        i = INDEX[key]
        here = got.at[i, :, columns(part, width)]
        return pltpu.make_async_remote_copy(
            src_ref=here, dst_ref=here, send_sem=send.at[i], recv_sem=recv.at[i],
            device_id=plane.neighbour(axis, d), device_id_type=BY_MESH,
        )

    started = []
    top = max(s[0] for s in STAGES)

    def when(stage):
        r, s, waits, starts = stage
        return (top - r - (0 if starts else 1), 2 - s)

    used = 0
    for r, s, keys, children in sorted(STAGES, key=when):
        half = (keys or children)[0][0]
        if not children:
            for key in keys:
                src = x.at[plane.slot(key[3]), half, :, columns(key[4], width)]
                copy = send_of(key, src)
                copy.start()
                started.append(copy)
            continue
        for child in children:
            recv_of(child).wait_recv()
        shard = keys[0][3] if keys else (0, 0)
        whole = [c for c in children if c[4] == 2]
        split = [c for c in children if c[4] != 2]
        for piece in range(2):
            cols = columns(piece, width)
            total = x[plane.slot(shard), half, :, cols]
            for child in whole + [c for c in split if c[4] == piece]:
                total = total + got[INDEX[child], :, cols]
            if keys:
                work[used, :, cols] = total
            else:
                out[half, :, cols] = total
        if keys:
            for key in keys:
                copy = send_of(key, work.at[used, :, columns(key[4], width)])
                copy.start()
                started.append(copy)
            used += 1
    for copy in started:
        copy.wait_send()


WORKS = sum(1 for _, _, waits, starts in STAGES if waits and starts)


def plane_scatter(x, collective_id):
    rows, width = x.shape
    piece = rows // (NY * NZ * 2)
    n = len(KEYS)
    out = pl.pallas_call(
        scatter_kernel,
        out_shape=jax.ShapeDtypeStruct((2, piece, width), x.dtype),
        in_specs=[pl.BlockSpec(memory_space=pltpu.VMEM)],
        out_specs=pl.BlockSpec(memory_space=pltpu.VMEM),
        scratch_shapes=[
            pltpu.VMEM((n, piece, width), x.dtype),
            pltpu.VMEM((WORKS, piece, width), x.dtype),
            pltpu.SemaphoreType.DMA((n,)),
            pltpu.SemaphoreType.DMA((n,)),
        ],
        compiler_params=pltpu.CompilerParams(
            collective_id=collective_id, has_side_effects=True, vmem_limit_bytes=48 << 20
        ),
        name="plane_scatter",
    )(x.reshape(NY * NZ, 2, piece, width))
    return out.reshape(2 * piece, width)


NX = 4


def row_sum_kernel(g, e, out, eff, met, epart, ehere, acc, got, work, send, recv):
    row = lax.axis_index("row")
    core = lax.rem(row, 2)
    x = lax.div(row, 2)
    other = 1 - core
    partner = {"row": x * 2 + other}

    def at(d):
        return {"row": wrap(x + d, NX) * 2 + core}

    def q(d):
        return wrap(x + d, NX)

    greet([partner, at(1), at(-1), at(2)])
    rows = g.shape[2]
    halves = (pl.ds(0, rows // 2), pl.ds(rows // 2, rows // 2))
    started = []
    ids = {}

    def copy(name, src, dst, device):
        i = ids.setdefault(name, len(ids))
        return pltpu.make_async_remote_copy(
            src_ref=src, dst_ref=dst, send_sem=send.at[i], recv_sem=recv.at[i],
            device_id=device, device_id_type=BY_MESH,
        )

    def go(c):
        c.start()
        started.append(c)

    order = (2, 1, -1, 0)
    for d in order:
        go(copy(("met", d), g.at[other, q(d)], met.at[q(d)], partner))
    go(copy("epart", e, epart.at[0], partner))
    for d in order:
        here = met.at[q(d)]
        copy(("met", d), here, here, partner).wait_recv()
        acc[q(d)] = g[core, q(d)] + met[q(d)]
        if d == 2:
            for s in DIRS:
                h = halves[part_of(s)]
                go(copy(("rs2", s), acc.at[q(2), h], got.at[part_of(s), pl.ds(0, rows // 2)], at(-s)))
        elif d != 0:
            s = -d
            h = halves[part_of(s)]
            dst = got.at[part_of(s), pl.ds(0, rows // 2)]
            copy(("rs2", s), dst, dst, at(s)).wait_recv()
            o = halves[1 - part_of(s)]
            work[part_of(s), h] = acc[q(d), h] + got[part_of(s), pl.ds(0, rows // 2)]
            work[part_of(s), o] = acc[q(d), o]
            go(copy(("rs1", s), work.at[part_of(s)], got.at[2 + part_of(s)], at(-s)))
    copy("epart", e, epart.at[0], partner).wait_recv()
    ehere[...] = e[...] + epart[0]
    for i, d in enumerate((2, 1, -1)):
        go(copy(("e", d), ehere, epart.at[1 + i], at(d)))
    for s in DIRS:
        dst = got.at[2 + part_of(s)]
        copy(("rs1", s), dst, dst, at(s)).wait_recv()
    mine = acc[q(0)] + got[2] + got[3]
    work[2] = mine
    for s in DIRS:
        go(copy(("ag1", s), work.at[2], out.at[core, q(0)], at(s)))
    go(copy(("hand", 0), work.at[2], out.at[core, q(0)], partner))
    out[core, q(0)] = mine
    for s in DIRS:
        block = out.at[core, q(-s)]
        copy(("ag1", s), block, block, at(-s)).wait_recv()
        h = halves[part_of(s)]
        piece = out.at[core, q(-s), h]
        go(copy(("ag2", s), piece, piece, at(s)))
        go(copy(("hand", -s), block, block, partner))
    for s in DIRS:
        piece = out.at[core, q(2), halves[part_of(s)]]
        copy(("ag2", s), piece, piece, at(-s)).wait_recv()
    block = out.at[core, q(2)]
    go(copy(("hand", 2), block, block, partner))
    total = ehere[...]
    for i, d in enumerate((2, 1, -1)):
        copy(("e", d), epart.at[1 + i], epart.at[1 + i], at(-d)).wait_recv()
        total = total + epart[1 + i]
    eff[...] = total
    for d in order:
        block = out.at[other, q(d)]
        copy(("hand", d), block, block, partner).wait_recv()
    for c in started:
        c.wait_send()


def row_sum(g, e, collective_id):
    rows, width = g.shape
    piece = rows // (2 * NX)
    sums, eff = pl.pallas_call(
        row_sum_kernel,
        out_shape=(
            jax.ShapeDtypeStruct((2, NX, piece, width), g.dtype),
            jax.ShapeDtypeStruct(e.shape, e.dtype),
        ),
        in_specs=[pl.BlockSpec(memory_space=pltpu.VMEM)] * 2,
        out_specs=(pl.BlockSpec(memory_space=pltpu.VMEM),) * 2,
        scratch_shapes=[
            pltpu.VMEM((NX, piece, width), g.dtype),
            pltpu.VMEM((4, *e.shape), e.dtype),
            pltpu.VMEM(e.shape, e.dtype),
            pltpu.VMEM((NX, piece, width), g.dtype),
            pltpu.VMEM((4, piece, width), g.dtype),
            pltpu.VMEM((3, piece, width), g.dtype),
            pltpu.SemaphoreType.DMA((20,)),
            pltpu.SemaphoreType.DMA((20,)),
        ],
        compiler_params=pltpu.CompilerParams(
            collective_id=collective_id, has_side_effects=True, vmem_limit_bytes=48 << 20
        ),
        name="row_sum",
    )(g.reshape(2, NX, piece, width), e)
    return sums.reshape(rows, width), eff


def deal_kernel(x, out, send, recv):
    row = lax.axis_index("row")
    core, xx = lax.rem(row, 2), lax.div(row, 2)
    y, z = lax.axis_index("col_0"), lax.axis_index("col_1")
    first = 4 * core
    deals = (y == xx) & (z >= first) & (z < first + 4)
    barrier = pltpu.get_barrier_semaphore()
    targets = [(dy, dz) for dy in range(NY) for dz in range(NZ) if (dy, dz) != (0, 0)]

    def me_at(dy, dz):
        return {"col_0": wrap(y + dy, NY), "col_1": wrap(z + dz, NZ)}

    for k in range(4):
        own = (y == xx) & (z == first + k)

        @pl.when(jnp.logical_not(own))
        def _():
            pl.semaphore_signal(
                barrier, inc=1, device_id={"col_0": xx, "col_1": first + k}, device_id_type=BY_MESH
            )

    @pl.when(deals)
    def _():
        for dy, dz in targets:
            pl.semaphore_signal(barrier, inc=1, device_id=me_at(dy, dz), device_id_type=BY_MESH)
        pl.semaphore_wait(barrier, len(targets) + 3)
        k = wrap(z - first, NZ)
        copies = []
        for i, (dy, dz) in enumerate(targets):
            ty, tz = wrap(y + dy, NY), wrap(z + dz, NZ)
            c = pltpu.make_async_remote_copy(
                src_ref=x.at[ty * NZ + tz], dst_ref=out.at[k], send_sem=send.at[i], recv_sem=recv.at[k],
                device_id={"col_0": ty, "col_1": tz}, device_id_type=BY_MESH,
            )
            c.start()
            copies.append(c)
        out[k] = x[y * NZ + z]
        for c in copies:
            c.wait_send()

    @pl.when(jnp.logical_not(deals))
    def _():
        pl.semaphore_wait(barrier, 4)

    for k in range(4):
        own = (y == xx) & (z == first + k)

        @pl.when(jnp.logical_not(own))
        def _():
            pltpu.make_async_remote_copy(
                src_ref=out.at[k], dst_ref=out.at[k], send_sem=send.at[0], recv_sem=recv.at[k],
                device_id={"col_0": xx, "col_1": first + k}, device_id_type=BY_MESH,
            ).wait_recv()


def deal(x, collective_id):
    rows, width = x.shape
    piece = rows // (NY * NZ)
    out = pl.pallas_call(
        deal_kernel,
        out_shape=jax.ShapeDtypeStruct((4, piece, width), x.dtype),
        in_specs=[pl.BlockSpec(memory_space=pltpu.VMEM)],
        out_specs=pl.BlockSpec(memory_space=pltpu.VMEM),
        scratch_shapes=[pltpu.SemaphoreType.DMA((31,)), pltpu.SemaphoreType.DMA((4,))],
        compiler_params=pltpu.CompilerParams(
            collective_id=collective_id, has_side_effects=True, vmem_limit_bytes=48 << 20
        ),
        name="deal",
    )(x.reshape(NY * NZ, piece, width))
    return jnp.moveaxis(out, 0, 1).reshape(piece, 4 * width)


def on_device(response, tile_map, band_offsets, prior_spectra, boot_counts, spectrum):
    row_place = lax.axis_index("row")
    col_place = lax.axis_index(COL)
    tiles_down, tiles_across = tile_map.shape
    tile_size = response.shape[0] // tiles_down
    measured = row_place * tiles_down + jnp.arange(tiles_down, dtype=jnp.int32)[:, None]
    truth = col_place * tiles_across + jnp.arange(tiles_across, dtype=jnp.int32)[None, :]
    inside = (truth >= measured + band_offsets[:, 0:1]) & (truth <= measured + band_offsets[:, 1:2])
    kept = (truth == measured) | inside & (tile_map == 1)
    expanded = jnp.repeat(jnp.repeat(kept, tile_size, 0), tile_size, 1)
    masked = jnp.where(expanded, response, jnp.zeros_like(response))
    replicas = prior_spectra.shape[0]
    dot = functools.partial(
        lax.dot_general, precision=lax.Precision.HIGH, preferred_element_type=jnp.float32
    )
    part = dot(prior_spectra, masked, (((1,), (1,)), ((), ())))
    folded = plane_scatter(part, 0)
    ratios = boot_counts.astype(jnp.float32) * spectrum[None, :] / folded
    fragment = plane_gather(ratios, 1)
    partial_value = dot(fragment, masked, (((1,), (0,)), ((), ())))
    column_sums = jnp.broadcast_to(jnp.sum(masked, axis=0)[None, :], (8, masked.shape[1]))
    summed, efficiency = row_sum(partial_value, column_sums, 2)
    unfolded = prior_spectra * summed / efficiency[0:1, :]
    centred = unfolded - jnp.mean(unfolded, axis=0)[None, :]
    own_rows = deal(centred, 3)
    covariance = dot(plane_gather(own_rows, 4), centred, (((0,), (0,)), ((), ())))
    return (covariance / (replicas - 1), unfolded)


def solution(mesh):
    torus = Mesh(mesh.devices.reshape(mesh.shape["row"], NY, NZ), ("row", "col_0", "col_1"))
    return jax.shard_map(
        on_device,
        mesh=torus,
        in_specs=(
            P("row", COL),
            P("row", COL),
            P("row", None),
            P(None, COL),
            P(COL, "row"),
            P("row"),
        ),
        out_specs=(P("row", COL), P(None, COL)),
        check_vma=False,
    )
```
